32 devices in a mesh: bank: 2 (over x), basis: 16 (over z, y, core).
Axes of the slice: x: 2, y: 2, z: 4, core: 2. Of those that a mesh axis runs over, the one named last changes fastest.
Arguments:
- strain: float32 [256, 4, 2, 128], P('basis'), may hold values from -6 to 6
- basis_vectors: bfloat16 [64, 256, 2, 128], P(('bank', 'basis')), parts along dimension 0, may hold values from -0.0234375 to 0.0234375
- coefficients: float32 [512, 2, 32], P(('bank', 'basis')), parts along dimension 0, may hold values from -0.75 to 0.75
- template_rows: int32 [512], P('bank'), parts along dimension 0, may hold values from 0 to 255
Outputs:
- snr_power: float32 [4, 512, 256, 256], P(None, 'bank', 'basis'), parts along dimension 1
The draws below stay inside these ranges and needn't reach their ends.
There are 2 independent parts, one for each index of `bank`. The reference program is written for one: setup_inputs(seed, part) draws one part's arguments, and reference() takes and returns one part's arrays. A program takes and returns all parts, laid end to end along the dimension named above; an argument that names none is the same for every part. Nothing has to cross between parts.
Inputs may be any that keep to these rules, and one draw needn't show every extreme that they name: template_rows[j] is the coefficient row of the j-th of the 256 rebuilt templates, the same for every sample.
All inputs are finite; a program needn't handle non-finite values.
Results may differ from the reference program's by a relative error of at most 0.0041.
Values may be sent and summed in bfloat16 or wider, within the bound.
A program may use at most 192 MiB of HBM per device.

```python
import jax
import jax.numpy as jnp
from jax import lax

SIDE = 256
SAMPLES = 65536
BASIS_VECS = 32
SEG = 4
TEMPLATES = 256
BANK_ROWS = 256
N_BASIS = 16


def with_ends(entries, own_key, least, high):
    longest = entries.shape.index(max(entries.shape))
    spots = []
    for shift in (0, 1):
        where = [jax.random.randint(jax.random.fold_in(own_key, axis), (), 0, length) for axis, length in enumerate(entries.shape)]
        where[longest] = (where[longest] + shift) % entries.shape[longest]
        spots.append(tuple(where))
    return entries.at[spots[0]].set(least).at[spots[1]].set(high)


def steps_of(rng, shape, split, low, high):
    gain, own = 1.0, jax.random.fold_in(rng, 6)
    for dim, shards_of in split:
        draws = jnp.exp(jax.random.uniform(jax.random.fold_in(own, dim), (shards_of,), jnp.float32, low / len(split), high / len(split)))
        gain = gain * jnp.repeat(draws, shape[dim] // shards_of).reshape([-1 if axis == dim else 1 for axis in range(len(shape))])
    return gain


def gaussian(own_key, dims, deviation, bound, cuts=(), dtype=jnp.bfloat16):
    entries = deviation * jax.random.normal(own_key, dims, jnp.float32)
    if cuts:
        entries = entries * steps_of(own_key, dims, cuts, -0.22, 0.18)
    return jnp.clip(entries, -bound, bound).astype(dtype)


def setup_inputs(seed: int = 0, part: int = 0) -> dict:
    keys = jax.random.split(jax.random.key(seed), 5)
    own_keys = jax.random.split(jax.random.fold_in(keys[4], part), 5)
    strain = gaussian(keys[0], (SIDE, SEG, 2, SIDE // 2), 1.0, 6.0, ((0, 16),), jnp.float32)
    basis_vectors = gaussian(own_keys[1], (BASIS_VECS, SIDE, 2, SIDE // 2), (SIDE * SIDE) ** -0.5, 0.0234375, ((0, 16),))
    coefficients = gaussian(own_keys[2], (BANK_ROWS, 2, BASIS_VECS), (2 * BASIS_VECS) ** -0.5, 0.75, ((0, 16),), jnp.float32)
    template_rows = with_ends(jax.random.randint(own_keys[3], (TEMPLATES,), 0, BANK_ROWS), jax.random.fold_in(own_keys[3], 1), 0, BANK_ROWS - 1).astype(jnp.int32)
    return {"strain": strain, "basis_vectors": basis_vectors, "coefficients": coefficients, "template_rows": template_rows}


highest = lax.Precision.HIGHEST


def rounded(values):
    return lax.optimization_barrier(values.astype(jnp.bfloat16)).astype(jnp.float32)


def reference(strain, basis_vectors, coefficients, template_rows):
    slice_len = SIDE // N_BASIS
    widened = basis_vectors.astype(jnp.float32)
    basis_re = widened[:, :, 0]
    basis_im = widened[:, :, 1]
    chosen = rounded(coefficients[template_rows])
    coeff_re = chosen[:, 0]
    coeff_im = chosen[:, 1]

    def owner_power(inputs):
        series_re, series_im = inputs
        flat_re = series_re.reshape(BASIS_VECS, slice_len * SIDE)
        flat_im = series_im.reshape(BASIS_VECS, slice_len * SIDE)
        rho_re = jnp.dot(coeff_re, flat_re, precision=highest) - jnp.dot(coeff_im, flat_im, precision=highest)
        rho_im = jnp.dot(coeff_re, flat_im, precision=highest) + jnp.dot(coeff_im, flat_re, precision=highest)
        return (rho_re * rho_re + rho_im * rho_im).reshape(TEMPLATES, slice_len, SIDE)

    def arrange(values):
        grid = values.reshape(BASIS_VECS, SIDE, SIDE)
        grid = jnp.transpose(grid, (0, 2, 1)).reshape(BASIS_VECS, N_BASIS, slice_len, SIDE)
        return jnp.transpose(grid, (1, 0, 2, 3))

    def one_segment(segment):
        strain_re = segment[:, 0]
        strain_im = segment[:, 1]
        prod_re = basis_re * strain_re + basis_im * strain_im
        prod_im = basis_re * strain_im - basis_im * strain_re
        spectrum = lax.complex(prod_re, prod_im)
        spectrum = jnp.transpose(spectrum, (0, 2, 1)).reshape(BASIS_VECS, SAMPLES // 2)
        spectrum = jnp.concatenate([spectrum, jnp.zeros_like(spectrum)], axis=1)
        series = jnp.fft.ifft(spectrum, axis=1) * SAMPLES
        grid_re = arrange(rounded(jnp.real(series)))
        grid_im = arrange(rounded(jnp.imag(series)))
        owners = lax.map(owner_power, (grid_re, grid_im))
        return jnp.transpose(owners, (1, 0, 2, 3)).reshape(TEMPLATES, SIDE, SIDE)

    return lax.map(one_segment, jnp.transpose(strain, (1, 0, 2, 3)))
```

```python
import functools
import math

import jax
import jax.numpy as jnp
import numpy as np
from jax import lax
from jax.experimental import pallas as pl
from jax.experimental.pallas import tpu as pltpu
from jax.sharding import PartitionSpec as P

highest = lax.Precision.HIGHEST


def rotation(left_index, right_index, period):
    turns = left_index * right_index % period
    angle = turns.astype(jnp.float32) * (2.0 * math.pi / period)
    return (jnp.cos(angle), jnp.sin(angle))


def complex_einsum(form, left_re, left_im, right_re, right_im):
    real_out = jnp.einsum(form, left_re, right_re, precision=highest) - jnp.einsum(
        form, left_im, right_im, precision=highest
    )
    imag_out = jnp.einsum(form, left_re, right_im, precision=highest) + jnp.einsum(
        form, left_im, right_re, precision=highest
    )
    return (real_out, imag_out)


def stack_rows(coeff_table, template_rows):
    chosen = coeff_table[template_rows].astype(jnp.bfloat16)
    return jnp.concatenate([chosen[:, 0], chosen[:, 1]], axis=0)


def rebuild(stacked, series_re, series_im):
    templates = stacked.shape[0] // 2
    left_sum = jnp.einsum("jk,sktu->sjtu", stacked, series_re, preferred_element_type=jnp.float32)
    right_sum = jnp.einsum("jk,sktu->sjtu", stacked, series_im, preferred_element_type=jnp.float32)
    rho_re = left_sum[:, :templates] - right_sum[:, templates:]
    rho_im = right_sum[:, :templates] + left_sum[:, templates:]
    return rho_re * rho_re + rho_im * rho_im


def shards_general(strain, basis_vectors, coefficients, template_rows):
    half_rows = strain.shape[3]
    side_len = 2 * half_rows
    samples = side_len * side_len
    freq_index = lax.broadcasted_iota(jnp.int32, (half_rows, side_len), 0)
    time_index = lax.broadcasted_iota(jnp.int32, (half_rows, side_len), 1)
    first_cos, first_sin = rotation(freq_index, time_index, side_len)
    column_index = lax.broadcasted_iota(jnp.int32, (side_len, side_len), 0)
    block_index = lax.broadcasted_iota(jnp.int32, (side_len, side_len), 1)
    second_cos, second_sin = rotation(column_index, block_index, side_len)
    coeff_table, whole_strain = (
        lax.all_gather(coefficients, "basis", axis=0, tiled=True),
        lax.all_gather(strain, "basis", axis=0, tiled=True),
    )
    stacked = stack_rows(coeff_table, template_rows)
    widened = basis_vectors.astype(jnp.float32)
    basis_re = widened[:, :, 0][None]
    basis_im = widened[:, :, 1][None]
    strain_re = jnp.transpose(whole_strain[:, :, 0], (1, 0, 2))[:, None]
    strain_im = jnp.transpose(whole_strain[:, :, 1], (1, 0, 2))[:, None]
    prod_re = basis_re * strain_re + basis_im * strain_im
    prod_im = basis_re * strain_im - basis_im * strain_re
    section_re, section_im = complex_einsum("skcr,rt->skct", prod_re, prod_im, first_cos, first_sin)
    twist_cos, twist_sin = rotation(column_index, block_index, samples)
    turned_re = section_re * twist_cos - section_im * twist_sin
    turned_im = section_re * twist_sin + section_im * twist_cos
    series_re, series_im = complex_einsum(
        "skct,cu->sktu", turned_re, turned_im, second_cos, second_sin
    )
    series_re = series_re.astype(jnp.bfloat16)
    series_im = series_im.astype(jnp.bfloat16)
    return rebuild(
        stacked,
        lax.all_to_all(series_re, "basis", split_axis=2, concat_axis=1, tiled=True),
        lax.all_to_all(series_im, "basis", split_axis=2, concat_axis=1, tiled=True),
    )


bf16 = jnp.bfloat16
f32 = jnp.float32
NT = (((1,), (1,)), ((), ()))
TN = (((0,), (0,)), ((), ()))


def split(values):
    high = values.astype(bf16)
    return high, (values - high.astype(f32)).astype(bf16)


def table(rows, columns, period):
    turns = np.outer(np.arange(rows), np.arange(columns)) % period
    angle = turns * (2.0 * math.pi / period)
    return np.cos(angle), np.sin(angle)


def halves(values):
    values = values.astype(np.float32)
    high = values.astype(bf16)
    return high, (values - high.astype(np.float32)).astype(bf16)


def exchange(n, segs, u_ref, strain_ref, coeff_ref, first_hi, first_lo, turn_ref, got_ref, table_ref,
             u_all, wide_re, wide_im, sect, packed, send_u, recv_u, send_c, recv_c, send_s, recv_s, own_sem):
    me = lax.axis_index("basis")
    cols = u_ref.shape[1] // n
    k_loc = u_ref.shape[0]
    side = u_ref.shape[1]
    half = side // 2
    n_k = k_loc * n
    res = side // n

    barrier = pltpu.get_barrier_semaphore()
    for off in range(1, n):
        pl.semaphore_signal(barrier, inc=1, device_id={"basis": lax.rem(me + off, n)},
                            device_id_type=pl.DeviceIdType.MESH)
    pl.semaphore_wait(barrier, n - 1)

    sends = []
    for off in range(1, n):
        peer = lax.rem(me + off, n)
        block = pl.ds(pl.multiple_of(peer * cols, cols), cols)
        sends.append(pltpu.make_async_remote_copy(
            u_ref.at[:, block], u_all.at[me], send_u.at[off], recv_u.at[off],
            device_id={"basis": peer}, device_id_type=pl.DeviceIdType.MESH))
        sends[-1].start()
    coeffs = []
    for off in range(1, n):
        peer = lax.rem(me + off, n)
        coeffs.append(pltpu.make_async_remote_copy(
            coeff_ref, table_ref.at[me], send_c.at[off], recv_c.at[off],
            device_id={"basis": peer}, device_id_type=pl.DeviceIdType.MESH))
        coeffs[-1].start()
    own_block = pl.ds(pl.multiple_of(me * cols, cols), cols)
    own_u = pltpu.make_async_copy(u_ref.at[:, own_block], u_all.at[me], own_sem.at[0])
    own_u.start()
    own_c = pltpu.make_async_copy(coeff_ref, table_ref.at[me], own_sem.at[1])
    own_c.start()
    own_u.wait()
    for copy in sends:
        copy.wait()

    wide = u_all[...].astype(f32).reshape(n_k * cols, side)
    wide_re[...] = wide[:, :half]
    wide_im[...] = wide[:, half:]
    for c in range(cols):
        u_re = wide_re[pl.ds(c, n_k, stride=cols), :]
        u_im = wide_im[pl.ds(c, n_k, stride=cols), :]
        parts = []
        for s in range(segs):
            row = c * segs + s
            d_re = strain_ref[row:row + 1, :half]
            d_im = strain_ref[row:row + 1, half:]
            parts.append(jnp.concatenate([u_re * d_re + u_im * d_im, u_re * d_im - u_im * d_re], axis=1))
        high, low = split(jnp.concatenate(parts, axis=0))
        out = lax.dot_general(first_hi[...], high, NT, preferred_element_type=f32)
        out += lax.dot_general(first_lo[...], high, NT, preferred_element_type=f32)
        out += lax.dot_general(first_hi[...], low, NT, preferred_element_type=f32)
        t_cos = turn_ref[:, c:c + 1]
        t_sin = turn_ref[:, cols + c:cols + c + 1]
        o_re, o_im = out[:side], out[side:]
        sect[0, pl.ds(c, side, stride=cols), :] = o_re * t_cos - o_im * t_sin
        sect[1, pl.ds(c, side, stride=cols), :] = o_re * t_sin + o_im * t_cos
    packed[...] = sect[...].astype(bf16).reshape(packed.shape)

    blocks = []
    for off in range(1, n):
        peer = lax.rem(me + off, n)
        blocks.append(pltpu.make_async_remote_copy(
            packed.at[:, pl.ds(peer * res, res)], got_ref.at[me], send_s.at[off], recv_s.at[off],
            device_id={"basis": peer}, device_id_type=pl.DeviceIdType.MESH))
        blocks[-1].start()
    own_s = pltpu.make_async_copy(packed.at[:, pl.ds(me * res, res)], got_ref.at[me], own_sem.at[2])
    own_s.start()
    own_c.wait()
    for copy in coeffs:
        copy.wait()
    own_s.wait()
    for copy in blocks:
        copy.wait()


def rebuild_kernel(segs, got_ref, table_ref, rows_ref, second_hi, second_lo, out_ref,
                   series, left_re, left_im, stage, out_sem):
    n, _, res, cols, wide = got_ref.shape
    side = n * cols
    n_k = wide // segs
    step_s = pl.program_id(0)
    step_j = pl.program_id(1)
    j_steps = pl.num_programs(1)
    j_block = out_ref.shape[1] // res // j_steps
    step = step_s * j_steps + step_j
    slot = lax.rem(step, 2)

    def writes(at_slot, at_s, at_j):
        height = j_block * res
        span = pl.ds(pl.multiple_of(at_j * height, height), height)
        return [pltpu.make_async_copy(stage.at[at_slot, h], out_ref.at[at_s, span, pl.ds(h * 128, 128)],
                                      out_sem.at[at_slot, h]) for h in range(side // 128)]

    @pl.when((step_s == 0) & (step_j == 0))
    def _():
        n_rows = table_ref.shape[0]
        lanes = lax.broadcasted_iota(jnp.int32, (rows_ref.shape[0], n_rows), 1)
        hot = jnp.where(lanes == rows_ref[...], 1.0, 0.0).astype(bf16)
        left = jnp.dot(hot, table_ref[...], preferred_element_type=f32).astype(bf16)
        left_re[...] = left[:, :2 * n_k]
        left_im[...] = left[:, 2 * n_k:]

        @pl.loop(0, res)
        def _(a):
            both = []
            for part in range(2):
                block = got_ref[:, part, a].reshape(side, wide)
                both.append(lax.dot_general(block, second_hi[...], TN, preferred_element_type=f32)
                            + lax.dot_general(block, second_lo[...], TN, preferred_element_type=f32))
            z_re = (both[0][:, :side] - both[1][:, side:]).astype(bf16)
            z_im = (both[0][:, side:] + both[1][:, :side]).astype(bf16)
            for s in range(segs):
                series[s, a, :n_k] = z_re[s * n_k:(s + 1) * n_k]
                series[s, a, n_k:] = z_im[s * n_k:(s + 1) * n_k]

    @pl.when(step >= 2)
    def _():
        for copy in writes(slot, 0, 0):
            copy.wait()

    rows = pl.ds(pl.multiple_of(step_j * j_block, j_block), j_block)
    l_re = left_re[rows, :]
    l_im = left_im[rows, :]
    for a in range(res):
        right = series[step_s, a]
        p_re = jnp.dot(l_re, right, preferred_element_type=f32)
        p_im = jnp.dot(l_im, right, preferred_element_type=f32)
        power = p_re * p_re + p_im * p_im
        for h in range(side // 128):
            stage[slot, h, pl.ds(a, j_block, stride=res), :] = power[:, h * 128:(h + 1) * 128]
    for copy in writes(slot, step_s, step_j):
        copy.start()

    @pl.when(step == pl.num_programs(0) * j_steps - 1)
    def _():
        for at_slot in range(2):
            for copy in writes(at_slot, 0, 0):
                copy.wait()


def shards(n, strain, basis_vectors, coefficients, template_rows):
    cols, segs, _, half = strain.shape
    side = 2 * half
    k_loc = basis_vectors.shape[0]
    n_k = k_loc * n
    res = side // n
    templates = template_rows.shape[0]
    wide = segs * n_k
    if cols % 16 or wide != 128 or n_k % 16 or coefficients.shape[0] % 16:
        return shards_general(strain, basis_vectors, coefficients, template_rows)
    samples = side * side
    cos1, sin1 = table(side, half, side)
    first_hi, first_lo = halves(np.block([[cos1, -sin1], [sin1, cos1]]))
    cos2, sin2 = table(side, side, side)
    second_hi, second_lo = halves(np.concatenate([cos2, sin2], axis=1))
    me = lax.axis_index("basis")
    column = me * cols + lax.broadcasted_iota(jnp.int32, (side, cols), 1)
    turns = column * lax.broadcasted_iota(jnp.int32, (side, cols), 0) % samples
    angle = turns.astype(f32) * (2.0 * math.pi / samples)
    turn = jnp.concatenate([jnp.cos(angle), jnp.sin(angle)], axis=1)
    c_re, c_im = coefficients[:, 0].astype(bf16), coefficients[:, 1].astype(bf16)
    packed_coeff = jnp.concatenate([c_re, -c_im, c_im, c_re], axis=1)
    rows_loc = coefficients.shape[0]
    u = basis_vectors.reshape(k_loc, side, side)
    d = strain.reshape(cols * segs, side)
    vmem = pl.BlockSpec(memory_space=pltpu.VMEM)
    hbm = pl.BlockSpec(memory_space=pl.ANY)
    got, coeff_table = pl.pallas_call(
        functools.partial(exchange, n, segs),
        out_shape=[jax.ShapeDtypeStruct((n, 2, res, cols, wide), bf16),
                   jax.ShapeDtypeStruct((n, rows_loc, 4 * n_k), bf16)],
        in_specs=[vmem] * 6,
        out_specs=[hbm, hbm],
        scratch_shapes=[
            pltpu.VMEM((n, k_loc, cols, side), bf16),
            pltpu.VMEM((n_k * cols, half), f32),
            pltpu.VMEM((n_k * cols, half), f32),
            pltpu.VMEM((2, side * cols, wide), f32),
            pltpu.VMEM((2, side, cols, wide), bf16),
        ] + [pltpu.SemaphoreType.DMA((n,))] * 6 + [pltpu.SemaphoreType.DMA((3,))],
        compiler_params=pltpu.CompilerParams(collective_id=0, has_side_effects=True),
    )(u, d, packed_coeff, first_hi, first_lo, turn)
    j_block = templates // 2
    power = pl.pallas_call(
        functools.partial(rebuild_kernel, segs),
        grid=(segs, templates // j_block),
        out_shape=jax.ShapeDtypeStruct((segs, templates * res, side), f32),
        in_specs=[vmem] * 5,
        out_specs=hbm,
        scratch_shapes=[
            pltpu.VMEM((segs, res, 2 * n_k, side), bf16),
            pltpu.VMEM((templates, 2 * n_k), bf16),
            pltpu.VMEM((templates, 2 * n_k), bf16),
            pltpu.VMEM((2, side // 128, j_block * res, 128), f32),
            pltpu.SemaphoreType.DMA((2, side // 128)),
        ],
    )(got, coeff_table.reshape(n * rows_loc, 4 * n_k), template_rows[:, None], second_hi, second_lo)
    return power.reshape(segs, templates, res, side)


def solution(mesh):
    in_specs = (
        P("basis", None, None, None),
        P(("bank", "basis"), None, None, None),
        P(("bank", "basis"), None, None),
        P("bank"),
    )
    out_specs = P(None, "bank", "basis", None)
    return jax.shard_map(functools.partial(shards, mesh.shape["basis"]), mesh=mesh, in_specs=in_specs, out_specs=out_specs, check_vma=False)
```

```python
import functools
import math

import jax
import jax.numpy as jnp
import numpy as np
from jax import lax
from jax.experimental import pallas as pl
from jax.experimental.pallas import tpu as pltpu
from jax.sharding import PartitionSpec as P

highest = lax.Precision.HIGHEST


def rotation(left_index, right_index, period):
    turns = left_index * right_index % period
    angle = turns.astype(jnp.float32) * (2.0 * math.pi / period)
    return (jnp.cos(angle), jnp.sin(angle))


def complex_einsum(form, left_re, left_im, right_re, right_im):
    real_out = jnp.einsum(form, left_re, right_re, precision=highest) - jnp.einsum(
        form, left_im, right_im, precision=highest
    )
    imag_out = jnp.einsum(form, left_re, right_im, precision=highest) + jnp.einsum(
        form, left_im, right_re, precision=highest
    )
    return (real_out, imag_out)


def stack_rows(coeff_table, template_rows):
    chosen = coeff_table[template_rows].astype(jnp.bfloat16)
    return jnp.concatenate([chosen[:, 0], chosen[:, 1]], axis=0)


def rebuild(stacked, series_re, series_im):
    templates = stacked.shape[0] // 2
    left_sum = jnp.einsum("jk,sktu->sjtu", stacked, series_re, preferred_element_type=jnp.float32)
    right_sum = jnp.einsum("jk,sktu->sjtu", stacked, series_im, preferred_element_type=jnp.float32)
    rho_re = left_sum[:, :templates] - right_sum[:, templates:]
    rho_im = right_sum[:, :templates] + left_sum[:, templates:]
    return rho_re * rho_re + rho_im * rho_im


def shards_general(strain, basis_vectors, coefficients, template_rows):
    half_rows = strain.shape[3]
    side_len = 2 * half_rows
    samples = side_len * side_len
    freq_index = lax.broadcasted_iota(jnp.int32, (half_rows, side_len), 0)
    time_index = lax.broadcasted_iota(jnp.int32, (half_rows, side_len), 1)
    first_cos, first_sin = rotation(freq_index, time_index, side_len)
    column_index = lax.broadcasted_iota(jnp.int32, (side_len, side_len), 0)
    block_index = lax.broadcasted_iota(jnp.int32, (side_len, side_len), 1)
    second_cos, second_sin = rotation(column_index, block_index, side_len)
    coeff_table, whole_strain = (
        lax.all_gather(coefficients, "basis", axis=0, tiled=True),
        lax.all_gather(strain, "basis", axis=0, tiled=True),
    )
    stacked = stack_rows(coeff_table, template_rows)
    widened = basis_vectors.astype(jnp.float32)
    basis_re = widened[:, :, 0][None]
    basis_im = widened[:, :, 1][None]
    strain_re = jnp.transpose(whole_strain[:, :, 0], (1, 0, 2))[:, None]
    strain_im = jnp.transpose(whole_strain[:, :, 1], (1, 0, 2))[:, None]
    prod_re = basis_re * strain_re + basis_im * strain_im
    prod_im = basis_re * strain_im - basis_im * strain_re
    section_re, section_im = complex_einsum("skcr,rt->skct", prod_re, prod_im, first_cos, first_sin)
    twist_cos, twist_sin = rotation(column_index, block_index, samples)
    turned_re = section_re * twist_cos - section_im * twist_sin
    turned_im = section_re * twist_sin + section_im * twist_cos
    series_re, series_im = complex_einsum(
        "skct,cu->sktu", turned_re, turned_im, second_cos, second_sin
    )
    series_re = series_re.astype(jnp.bfloat16)
    series_im = series_im.astype(jnp.bfloat16)
    return rebuild(
        stacked,
        lax.all_to_all(series_re, "basis", split_axis=2, concat_axis=1, tiled=True),
        lax.all_to_all(series_im, "basis", split_axis=2, concat_axis=1, tiled=True),
    )


bf16 = jnp.bfloat16
f32 = jnp.float32
NT = (((1,), (1,)), ((), ()))
TN = (((0,), (0,)), ((), ()))


def split(values):
    high = values.astype(bf16)
    return high, (values - high.astype(f32)).astype(bf16)


def table(rows, columns, period):
    turns = np.outer(np.arange(rows), np.arange(columns)) % period
    angle = turns * (2.0 * math.pi / period)
    return np.cos(angle), np.sin(angle)


def halves(values):
    values = values.astype(np.float32)
    high = values.astype(bf16)
    return high, (values - high.astype(np.float32)).astype(bf16)


def exchange(n, group, segs, u_ref, strain_ref, coeff_ref, first_hi, first_lo, turn_ref, got_ref, table_ref,
             u_all, strain_all, wide_re, wide_im, sect, packed, left_hi, left_lo,
             send_u, recv_u, send_z, recv_z, send_d, recv_d, send_c, recv_c, send_s, recv_s, own_sem):
    me = lax.axis_index("basis")
    layers = n // group
    layer = me // group
    lane = lax.rem(me, group)
    k_loc, side = u_ref.shape[0], u_ref.shape[1]
    cols = side // n
    half = side // 2
    n_k = k_loc * n
    res = side // n
    near = group * res

    def remote(src, dst, send, recv, peer):
        return pltpu.make_async_remote_copy(src, dst, send, recv, device_id={"basis": peer},
                                            device_id_type=pl.DeviceIdType.MESH)

    def mate(off):
        return lax.rem(lane + off, group)

    def columns(q, owner):
        return pl.ds(pl.multiple_of((q * group + owner) * cols, cols), cols)

    def swap_u(off, q):
        to = mate(off)
        return remote(u_ref.at[:, columns(q, to)], u_all.at[q, layer, lane], send_u.at[off, q], recv_u.at[off, q],
                      layer * group + to)

    def swap_s(off, q):
        to = mate(off)
        rows = pl.ds(pl.multiple_of(to * res, res), res)
        return remote(packed.at[q, :, rows], got_ref.at[q * group + lane], send_s.at[off, q], recv_s.at[off, q],
                      layer * group + to)

    def keep_u(q):
        return pltpu.make_async_copy(u_ref.at[:, columns(q, lane)], u_all.at[q, layer, lane], own_sem.at[0, q])

    def keep_s(q):
        rows = pl.ds(pl.multiple_of(lane * res, res), res)
        return pltpu.make_async_copy(packed.at[q, :, rows], got_ref.at[q * group + lane], own_sem.at[1, q])

    def pass_u(q, origin, way):
        return remote(u_all.at[q, origin], u_all.at[q, origin], send_z.at[q, origin, way], recv_z.at[q, origin],
                      me + (2 * way - 1) * group)

    def pass_d(origin, way):
        return remote(strain_all.at[origin], strain_all.at[origin], send_d.at[origin, way], recv_d.at[origin],
                      me + (2 * way - 1) * group)

    def share_c(off):
        return remote(coeff_ref, table_ref.at[me], send_c.at[off], recv_c.at[off], lax.rem(me + off, n))

    def towards(way):
        return layer < layers - 1 if way else layer > 0

    def relay(copy_of):
        for dist in range(1, layers):
            for way in range(2):
                origin = layer - dist if way else layer + dist

                @pl.when((origin >= 0) & (origin < layers))
                def _():
                    copy_of(origin, 0).wait_recv()

                    @pl.when(towards(way))
                    def _():
                        copy_of(origin, way).start()

    def drain(copy_of):
        for origin in range(layers):
            for way in range(2):
                sent = origin <= layer if way else origin >= layer

                @pl.when(towards(way) & sent)
                def _():
                    copy_of(origin, way).wait_send()

    def launch(q):
        keep_u(q).wait()
        for off in range(1, group):
            swap_u(off, q).wait_recv()
        for way in range(2):
            @pl.when(towards(way))
            def _():
                pass_u(q, layer, way).start()

    barrier = pltpu.get_barrier_semaphore()
    for off in range(1, n):
        pl.semaphore_signal(barrier, inc=1, device_id={"basis": lax.rem(me + off, n)},
                            device_id_type=pl.DeviceIdType.MESH)
    own_d = pltpu.make_async_copy(strain_ref, strain_all.at[layer], own_sem.at[2, 0])
    own_d.start()
    own_c = pltpu.make_async_copy(coeff_ref, table_ref.at[me], own_sem.at[2, 1])
    own_c.start()
    for q in range(layers):
        keep_u(q).start()
    own_d.wait()
    pl.semaphore_wait(barrier, n - 1)
    for q in range(layers):
        for off in range(1, group):
            swap_u(off, q).start()
    for way in range(2):
        @pl.when(towards(way))
        def _():
            pass_d(layer, way).start()
    for off in range(1, n):
        share_c(off).start()
    for part in range(2):
        rows = pl.ds(pl.multiple_of(part * side + layer * near, near), near)
        left_hi[part * near:(part + 1) * near, :] = first_hi[rows, :]
        left_lo[part * near:(part + 1) * near, :] = first_lo[rows, :]
    launch(0)
    relay(pass_d)
    launch(1)

    @pl.loop(0, layers)
    def _(q):
        relay(functools.partial(pass_u, q))

        @pl.when(q + 2 < layers)
        def _():
            launch(q + 2)

        wide = u_all[q].astype(f32).reshape(n_k * cols, side)
        wide_re[...] = wide[:, :half]
        wide_im[...] = wide[:, half:]
        turn = turn_ref[q]
        for c in range(cols):
            u_re = wide_re[pl.ds(c, n_k, stride=cols), :]
            u_im = wide_im[pl.ds(c, n_k, stride=cols), :]
            parts = []
            for s in range(segs):
                d_row = strain_all[q, c * segs + s:c * segs + s + 1, :]
                d_re, d_im = d_row[:, :half], d_row[:, half:]
                parts.append(jnp.concatenate([u_re * d_re + u_im * d_im, u_re * d_im - u_im * d_re], axis=1))
            high, low = split(jnp.concatenate(parts, axis=0))
            out = lax.dot_general(left_hi[...], high, NT, preferred_element_type=f32)
            out += lax.dot_general(left_lo[...], high, NT, preferred_element_type=f32)
            out += lax.dot_general(left_hi[...], low, NT, preferred_element_type=f32)
            t_cos = turn[:, c:c + 1]
            t_sin = turn[:, cols + c:cols + c + 1]
            o_re, o_im = out[:near], out[near:]
            sect[0, pl.ds(c, near, stride=cols), :] = o_re * t_cos - o_im * t_sin
            sect[1, pl.ds(c, near, stride=cols), :] = o_re * t_sin + o_im * t_cos
        packed[q] = sect[...].astype(bf16).reshape(packed.shape[1:])
        for off in range(1, group):
            swap_s(off, q).start()
        keep_s(q).start()

    own_c.wait()
    for off in range(1, n):
        share_c(off).wait()
    drain(pass_d)

    @pl.loop(0, layers)
    def _(q):
        drain(functools.partial(pass_u, q))
        keep_s(q).wait()
        for off in range(1, group):
            swap_u(off, q).wait_send()
            swap_s(off, q).wait()


def rebuild_kernel(segs, got_ref, table_ref, rows_ref, second_hi, second_lo, out_ref,
                   series, left_re, left_im, stage, out_sem):
    n, _, res, cols, wide = got_ref.shape
    side = n * cols
    n_k = wide // segs
    step_s = pl.program_id(0)
    step_j = pl.program_id(1)
    j_steps = pl.num_programs(1)
    j_block = out_ref.shape[1] // res // j_steps
    step = step_s * j_steps + step_j
    slot = lax.rem(step, 2)

    def writes(at_slot, at_s, at_j):
        height = j_block * res
        span = pl.ds(pl.multiple_of(at_j * height, height), height)
        return [pltpu.make_async_copy(stage.at[at_slot, h], out_ref.at[at_s, span, pl.ds(h * 128, 128)],
                                      out_sem.at[at_slot, h]) for h in range(side // 128)]

    @pl.when((step_s == 0) & (step_j == 0))
    def _():
        n_rows = table_ref.shape[0]
        index = lax.broadcasted_iota(jnp.int32, (n_rows, rows_ref.shape[1]), 0)
        hot = jnp.where(index == rows_ref[...], 1.0, 0.0).astype(bf16)
        left = lax.dot_general(hot, table_ref[...], TN, preferred_element_type=f32).astype(bf16)
        left_re[...] = left[:, :2 * n_k]
        left_im[...] = left[:, 2 * n_k:]

        @pl.loop(0, res)
        def _(a):
            both = []
            for part in range(2):
                block = got_ref[:, part, a].reshape(side, wide)
                both.append(lax.dot_general(block, second_hi[...], TN, preferred_element_type=f32)
                            + lax.dot_general(block, second_lo[...], TN, preferred_element_type=f32))
            z_re = (both[0][:, :side] - both[1][:, side:]).astype(bf16)
            z_im = (both[0][:, side:] + both[1][:, :side]).astype(bf16)
            for s in range(segs):
                series[s, a, :n_k] = z_re[s * n_k:(s + 1) * n_k]
                series[s, a, n_k:] = z_im[s * n_k:(s + 1) * n_k]

    @pl.when(step >= 2)
    def _():
        for copy in writes(slot, 0, 0):
            copy.wait()

    rows = pl.ds(pl.multiple_of(step_j * j_block, j_block), j_block)
    l_re = left_re[rows, :]
    l_im = left_im[rows, :]
    for a in range(res):
        right = series[step_s, a]
        p_re = jnp.dot(l_re, right, preferred_element_type=f32)
        p_im = jnp.dot(l_im, right, preferred_element_type=f32)
        power = p_re * p_re + p_im * p_im
        for h in range(side // 128):
            stage[slot, h, pl.ds(a, j_block, stride=res), :] = power[:, h * 128:(h + 1) * 128]
    for copy in writes(slot, step_s, step_j):
        copy.start()

    @pl.when(step == pl.num_programs(0) * j_steps - 1)
    def _():
        for at_slot in range(2):
            for copy in writes(at_slot, 0, 0):
                copy.wait()


def shards(n, strain, basis_vectors, coefficients, template_rows):
    cols, segs, _, half = strain.shape
    side = 2 * half
    k_loc = basis_vectors.shape[0]
    n_k = k_loc * n
    res = side // n
    templates = template_rows.shape[0]
    wide = segs * n_k
    if cols % 16 or wide != 128 or n_k % 16 or coefficients.shape[0] % 16 or math.isqrt(n) ** 2 != n:
        return shards_general(strain, basis_vectors, coefficients, template_rows)
    samples = side * side
    cos1, sin1 = table(side, half, side)
    first_hi, first_lo = halves(np.block([[cos1, -sin1], [sin1, cos1]]))
    cos2, sin2 = table(side, side, side)
    second_hi, second_lo = halves(np.concatenate([cos2, sin2], axis=1))
    me = lax.axis_index("basis")
    group = math.isqrt(n)
    layers = n // group
    grid = (layers, group * res, cols)
    lane = me % group
    column = (lax.broadcasted_iota(jnp.int32, grid, 0) * group + lane) * cols + lax.broadcasted_iota(jnp.int32, grid, 2)
    residue = me // group * group * res + lax.broadcasted_iota(jnp.int32, grid, 1)
    angle = (column * residue % samples).astype(f32) * (2.0 * math.pi / samples)
    turn = jnp.concatenate([jnp.cos(angle), jnp.sin(angle)], axis=2)
    c_re, c_im = coefficients[:, 0].astype(bf16), coefficients[:, 1].astype(bf16)
    packed_coeff = jnp.concatenate([c_re, -c_im, c_im, c_re], axis=1)
    rows_loc = coefficients.shape[0]
    u = basis_vectors.reshape(k_loc, side, side)
    d = strain.reshape(cols * segs, side)
    vmem = pl.BlockSpec(memory_space=pltpu.VMEM)
    hbm = pl.BlockSpec(memory_space=pl.ANY)
    got, coeff_table = pl.pallas_call(
        functools.partial(exchange, n, group, segs),
        out_shape=[jax.ShapeDtypeStruct((n, 2, res, cols, wide), bf16),
                   jax.ShapeDtypeStruct((n, rows_loc, 4 * n_k), bf16)],
        in_specs=[vmem] * 6,
        out_specs=[hbm, hbm],
        scratch_shapes=[
            pltpu.VMEM((layers, layers, group, k_loc, cols, side), bf16),
            pltpu.VMEM((layers, cols * segs, side), f32),
            pltpu.VMEM((n_k * cols, half), f32),
            pltpu.VMEM((n_k * cols, half), f32),
            pltpu.VMEM((2, group * res * cols, wide), f32),
            pltpu.VMEM((layers, 2, group * res, cols, wide), bf16),
            pltpu.VMEM((2 * group * res, side), bf16),
            pltpu.VMEM((2 * group * res, side), bf16),
        ] + [pltpu.SemaphoreType.DMA(dims) for dims in (
            (group, layers), (group, layers), (layers, layers, 2), (layers, layers), (layers, 2), (layers,),
            (n,), (n,), (group, layers), (group, layers), (3, layers))],
        compiler_params=pltpu.CompilerParams(collective_id=0, has_side_effects=True),
    )(u, d, packed_coeff, first_hi, first_lo, turn)
    j_block = templates // 2
    power = pl.pallas_call(
        functools.partial(rebuild_kernel, segs),
        grid=(segs, templates // j_block),
        out_shape=jax.ShapeDtypeStruct((segs, templates * res, side), f32),
        in_specs=[vmem] * 5,
        out_specs=hbm,
        scratch_shapes=[
            pltpu.VMEM((segs, res, 2 * n_k, side), bf16),
            pltpu.VMEM((templates, 2 * n_k), bf16),
            pltpu.VMEM((templates, 2 * n_k), bf16),
            pltpu.VMEM((2, side // 128, j_block * res, 128), f32),
            pltpu.SemaphoreType.DMA((2, side // 128)),
        ],
    )(got, coeff_table.reshape(n * rows_loc, 4 * n_k), template_rows[None], second_hi, second_lo)
    return power.reshape(segs, templates, res, side)


def solution(mesh):
    in_specs = (
        P("basis", None, None, None),
        P(("bank", "basis"), None, None, None),
        P(("bank", "basis"), None, None),
        P("bank"),
    )
    out_specs = P(None, "bank", "basis", None)
    return jax.shard_map(functools.partial(shards, mesh.shape["basis"]), mesh=mesh, in_specs=in_specs, out_specs=out_specs, check_vma=False)
```

```python
import functools
import math

import jax
import jax.numpy as jnp
import numpy as np
from jax import lax
from jax.experimental import pallas as pl
from jax.experimental.pallas import tpu as pltpu
from jax.sharding import PartitionSpec as P

highest = lax.Precision.HIGHEST


def rotation(left_index, right_index, period):
    turns = left_index * right_index % period
    angle = turns.astype(jnp.float32) * (2.0 * math.pi / period)
    return (jnp.cos(angle), jnp.sin(angle))


def complex_einsum(form, left_re, left_im, right_re, right_im):
    real_out = jnp.einsum(form, left_re, right_re, precision=highest) - jnp.einsum(
        form, left_im, right_im, precision=highest
    )
    imag_out = jnp.einsum(form, left_re, right_im, precision=highest) + jnp.einsum(
        form, left_im, right_re, precision=highest
    )
    return (real_out, imag_out)


def stack_rows(coeff_table, template_rows):
    chosen = coeff_table[template_rows].astype(jnp.bfloat16)
    return jnp.concatenate([chosen[:, 0], chosen[:, 1]], axis=0)


def rebuild(stacked, series_re, series_im):
    templates = stacked.shape[0] // 2
    left_sum = jnp.einsum("jk,sktu->sjtu", stacked, series_re, preferred_element_type=jnp.float32)
    right_sum = jnp.einsum("jk,sktu->sjtu", stacked, series_im, preferred_element_type=jnp.float32)
    rho_re = left_sum[:, :templates] - right_sum[:, templates:]
    rho_im = right_sum[:, :templates] + left_sum[:, templates:]
    return rho_re * rho_re + rho_im * rho_im


def shards_general(strain, basis_vectors, coefficients, template_rows):
    half_rows = strain.shape[3]
    side_len = 2 * half_rows
    samples = side_len * side_len
    freq_index = lax.broadcasted_iota(jnp.int32, (half_rows, side_len), 0)
    time_index = lax.broadcasted_iota(jnp.int32, (half_rows, side_len), 1)
    first_cos, first_sin = rotation(freq_index, time_index, side_len)
    column_index = lax.broadcasted_iota(jnp.int32, (side_len, side_len), 0)
    block_index = lax.broadcasted_iota(jnp.int32, (side_len, side_len), 1)
    second_cos, second_sin = rotation(column_index, block_index, side_len)
    coeff_table, whole_strain = (
        lax.all_gather(coefficients, "basis", axis=0, tiled=True),
        lax.all_gather(strain, "basis", axis=0, tiled=True),
    )
    stacked = stack_rows(coeff_table, template_rows)
    widened = basis_vectors.astype(jnp.float32)
    basis_re = widened[:, :, 0][None]
    basis_im = widened[:, :, 1][None]
    strain_re = jnp.transpose(whole_strain[:, :, 0], (1, 0, 2))[:, None]
    strain_im = jnp.transpose(whole_strain[:, :, 1], (1, 0, 2))[:, None]
    prod_re = basis_re * strain_re + basis_im * strain_im
    prod_im = basis_re * strain_im - basis_im * strain_re
    section_re, section_im = complex_einsum("skcr,rt->skct", prod_re, prod_im, first_cos, first_sin)
    twist_cos, twist_sin = rotation(column_index, block_index, samples)
    turned_re = section_re * twist_cos - section_im * twist_sin
    turned_im = section_re * twist_sin + section_im * twist_cos
    series_re, series_im = complex_einsum(
        "skct,cu->sktu", turned_re, turned_im, second_cos, second_sin
    )
    series_re = series_re.astype(jnp.bfloat16)
    series_im = series_im.astype(jnp.bfloat16)
    return rebuild(
        stacked,
        lax.all_to_all(series_re, "basis", split_axis=2, concat_axis=1, tiled=True),
        lax.all_to_all(series_im, "basis", split_axis=2, concat_axis=1, tiled=True),
    )


bf16 = jnp.bfloat16
f32 = jnp.float32
NT = (((1,), (1,)), ((), ()))
TN = (((0,), (0,)), ((), ()))


def split(values):
    high = values.astype(bf16)
    return high, (values - high.astype(f32)).astype(bf16)


def table(rows, columns, period):
    turns = np.outer(np.arange(rows), np.arange(columns)) % period
    angle = turns * (2.0 * math.pi / period)
    return np.cos(angle), np.sin(angle)


def halves(values):
    values = values.astype(np.float32)
    high = values.astype(bf16)
    return high, (values - high.astype(np.float32)).astype(bf16)


def exchange(n, group, segs, u_ref, strain_ref, coeff_ref, first_hi, first_lo, turn_ref, got_ref, table_ref,
             u_all, strain_all, wide_re, wide_im, sect, packed, left_hi, left_lo,
             send_u, recv_u, send_z, recv_z, send_d, recv_d, send_c, recv_c, send_s, recv_s, own_sem):
    me = lax.axis_index("basis")
    layers = n // group
    layer = me // group
    lane = lax.rem(me, group)
    k_loc, side = u_ref.shape[0], u_ref.shape[1]
    cols = side // n
    half = side // 2
    n_k = k_loc * n
    res = side // n
    near = group * res

    def remote(src, dst, send, recv, peer):
        return pltpu.make_async_remote_copy(src, dst, send, recv, device_id={"basis": peer},
                                            device_id_type=pl.DeviceIdType.MESH)

    def mate(off):
        return lax.rem(lane + off, group)

    def columns(q, owner):
        return pl.ds(pl.multiple_of((q * group + owner) * cols, cols), cols)

    def swap_u(off, q):
        to = mate(off)
        return remote(u_ref.at[:, columns(q, to)], u_all.at[q, layer, lane], send_u.at[off, q], recv_u.at[off, q],
                      layer * group + to)

    def swap_s(off, q):
        to = mate(off)
        rows = pl.ds(pl.multiple_of(to * res, res), res)
        return remote(packed.at[q, :, rows], got_ref.at[q * group + lane], send_s.at[off, q], recv_s.at[off, q],
                      layer * group + to)

    def keep_u(q):
        return pltpu.make_async_copy(u_ref.at[:, columns(q, lane)], u_all.at[q, layer, lane], own_sem.at[0, q])

    def keep_s(q):
        rows = pl.ds(pl.multiple_of(lane * res, res), res)
        return pltpu.make_async_copy(packed.at[q, :, rows], got_ref.at[q * group + lane], own_sem.at[1, q])

    def pass_u(q, origin, way):
        return remote(u_all.at[q, origin], u_all.at[q, origin], send_z.at[q, origin, way], recv_z.at[q, origin],
                      me + (2 * way - 1) * group)

    def pass_d(origin, way):
        return remote(strain_all.at[origin], strain_all.at[origin], send_d.at[origin, way], recv_d.at[origin],
                      me + (2 * way - 1) * group)

    def share_c(off):
        return remote(coeff_ref, table_ref.at[me], send_c.at[off], recv_c.at[off], lax.rem(me + off, n))

    def towards(way):
        return layer < layers - 1 if way else layer > 0

    def relay(copy_of):
        for dist in range(1, layers):
            for way in range(2):
                origin = layer - dist if way else layer + dist

                @pl.when((origin >= 0) & (origin < layers))
                def _():
                    copy_of(origin, 0).wait_recv()

                    @pl.when(towards(way))
                    def _():
                        copy_of(origin, way).start()

    def drain(copy_of):
        for origin in range(layers):
            for way in range(2):
                sent = origin <= layer if way else origin >= layer

                @pl.when(towards(way) & sent)
                def _():
                    copy_of(origin, way).wait_send()

    def launch(q):
        keep_u(q).wait()
        for off in range(1, group):
            swap_u(off, q).wait_recv()
        for way in range(2):
            @pl.when(towards(way) & (layer == q))
            def _():
                pass_d(layer, way).start()

            @pl.when(towards(way))
            def _():
                pass_u(q, layer, way).start()

    barrier = pltpu.get_barrier_semaphore()
    for off in range(1, n):
        pl.semaphore_signal(barrier, inc=1, device_id={"basis": lax.rem(me + off, n)},
                            device_id_type=pl.DeviceIdType.MESH)
    own_d = pltpu.make_async_copy(strain_ref, strain_all.at[layer], own_sem.at[2, 0])
    own_d.start()
    own_c = pltpu.make_async_copy(coeff_ref, table_ref.at[me], own_sem.at[2, 1])
    own_c.start()
    for q in range(layers):
        keep_u(q).start()
    own_d.wait()
    pl.semaphore_wait(barrier, n - 1)
    for q in range(layers):
        for off in range(1, group):
            swap_u(off, q).start()
    for part in range(2):
        rows = pl.ds(pl.multiple_of(part * side + layer * near, near), near)
        left_hi[part * near:(part + 1) * near, :] = first_hi[rows, :]
        left_lo[part * near:(part + 1) * near, :] = first_lo[rows, :]
    launch(0)
    for off in range(1, n):
        share_c(off).start()
    launch(1)

    @pl.loop(0, layers)
    def _(q):
        @pl.when(layer != q)
        def _():
            pass_d(q, 0).wait_recv()
            for way in range(2):
                ahead = layer > q if way else layer < q

                @pl.when(towards(way) & ahead)
                def _():
                    pass_d(q, way).start()

        relay(functools.partial(pass_u, q))

        @pl.when(q + 2 < layers)
        def _():
            launch(q + 2)

        wide = u_all[q].astype(f32).reshape(n_k * cols, side)
        wide_re[...] = wide[:, :half]
        wide_im[...] = wide[:, half:]
        turn = turn_ref[q]
        strain_q = strain_all[q].astype(f32)
        for c in range(cols):
            u_re = wide_re[pl.ds(c, n_k, stride=cols), :]
            u_im = wide_im[pl.ds(c, n_k, stride=cols), :]
            parts = []
            for s in range(segs):
                row = c * segs + s
                d_re, d_im = strain_q[row:row + 1, :half], strain_q[row:row + 1, half:]
                parts.append(jnp.concatenate([u_re * d_re + u_im * d_im, u_re * d_im - u_im * d_re], axis=1))
            high, low = split(jnp.concatenate(parts, axis=0))
            out = lax.dot_general(left_hi[...], high, NT, preferred_element_type=f32)
            out += lax.dot_general(left_lo[...], high, NT, preferred_element_type=f32)
            out += lax.dot_general(left_hi[...], low, NT, preferred_element_type=f32)
            t_cos = turn[:, c:c + 1]
            t_sin = turn[:, cols + c:cols + c + 1]
            o_re, o_im = out[:near], out[near:]
            sect[0, pl.ds(c, near, stride=cols), :] = o_re * t_cos - o_im * t_sin
            sect[1, pl.ds(c, near, stride=cols), :] = o_re * t_sin + o_im * t_cos
        packed[q] = sect[...].astype(bf16).reshape(packed.shape[1:])
        for off in range(1, group):
            swap_s(off, q).start()
        keep_s(q).start()

    own_c.wait()
    for off in range(1, n):
        share_c(off).wait()
    drain(pass_d)

    @pl.loop(0, layers)
    def _(q):
        drain(functools.partial(pass_u, q))
        keep_s(q).wait()
        for off in range(1, group):
            swap_u(off, q).wait_send()
            swap_s(off, q).wait()


def rebuild_kernel(segs, got_ref, table_ref, rows_ref, second_hi, second_lo, out_ref, series, left, stage, out_sem):
    n, _, res, cols, wide = got_ref.shape
    side = n * cols
    n_k = wide // segs
    templates = rows_ref.shape[1]
    tile = stage.shape[2] // templates
    batch = tile // 2
    step_a, step_s = pl.program_id(0), pl.program_id(1)
    step = step_a * segs + step_s
    slot = lax.rem(step, 2)

    def writes(at_slot, at_a, at_s):
        span = pl.ds(pl.multiple_of(at_a * tile, tile), tile)
        return [pltpu.make_async_copy(stage.at[at_slot, h].reshape(templates, tile, 128),
                                      out_ref.at[at_s, :, span, pl.ds(h * 128, 128)],
                                      out_sem.at[at_slot, h]) for h in range(side // 128)]

    def second(first):
        both = []
        for part in range(2):
            block = jnp.concatenate([got_ref[:, part, first + i].reshape(side, wide) for i in range(batch)], axis=1)
            both.append(lax.dot_general(block, second_hi[...], TN, preferred_element_type=f32)
                        + lax.dot_general(block, second_lo[...], TN, preferred_element_type=f32))
        z_re = (both[0][:, :side] - both[1][:, side:]).astype(bf16)
        z_im = (both[0][:, side:] + both[1][:, :side]).astype(bf16)
        for i in range(batch):
            for s in range(segs):
                rows = slice(i * wide + s * n_k, i * wide + (s + 1) * n_k)
                series[s, first + i, :n_k] = z_re[rows]
                series[s, first + i, n_k:] = z_im[rows]

    @pl.when(step == 0)
    def _():
        index = lax.broadcasted_iota(jnp.int32, (table_ref.shape[0], templates), 0)
        hot = jnp.where(index == rows_ref[...], 1.0, 0.0).astype(bf16)
        picked = lax.dot_general(hot, table_ref[...], TN, preferred_element_type=f32).astype(bf16)
        left[:templates] = picked[:, :2 * n_k]
        left[templates:] = picked[:, 2 * n_k:]

        @pl.loop(0, 2)
        def _(i):
            second(i * batch)

    @pl.when((step_s < 2) & (step_a < pl.num_programs(0) - 1))
    def _():
        second((step_a + 1) * tile + step_s * batch)

    @pl.when(step >= 2)
    def _():
        for copy in writes(slot, 0, 0):
            copy.wait()

    for a in range(tile):
        rho = jnp.dot(left[...], series[step_s, step_a * tile + a], preferred_element_type=f32)
        p_re, p_im = rho[:templates], rho[templates:]
        power = p_re * p_re + p_im * p_im
        for h in range(side // 128):
            stage[slot, h, pl.ds(a, templates, stride=tile), :] = power[:, h * 128:(h + 1) * 128]
    for copy in writes(slot, step_a, step_s):
        copy.start()

    @pl.when(step == pl.num_programs(0) * segs - 1)
    def _():
        for at_slot in range(2):
            for copy in writes(at_slot, 0, 0):
                copy.wait()


def shards(n, strain, basis_vectors, coefficients, template_rows):
    cols, segs, _, half = strain.shape
    side = 2 * half
    k_loc = basis_vectors.shape[0]
    n_k = k_loc * n
    res = side // n
    templates = template_rows.shape[0]
    wide = segs * n_k
    if cols % 16 or segs < 2 or wide != 128 or n_k % 16 or coefficients.shape[0] % 16 or math.isqrt(n) ** 2 != n:
        return shards_general(strain, basis_vectors, coefficients, template_rows)
    samples = side * side
    cos1, sin1 = table(side, half, side)
    first_hi, first_lo = halves(np.block([[cos1, -sin1], [sin1, cos1]]))
    cos2, sin2 = table(side, side, side)
    second_hi, second_lo = halves(np.concatenate([cos2, sin2], axis=1))
    me = lax.axis_index("basis")
    group = math.isqrt(n)
    layers = n // group
    grid = (layers, group * res, cols)
    lane = me % group
    column = (lax.broadcasted_iota(jnp.int32, grid, 0) * group + lane) * cols + lax.broadcasted_iota(jnp.int32, grid, 2)
    residue = me // group * group * res + lax.broadcasted_iota(jnp.int32, grid, 1)
    angle = (column * residue % samples).astype(f32) * (2.0 * math.pi / samples)
    turn = jnp.concatenate([jnp.cos(angle), jnp.sin(angle)], axis=2)
    c_re, c_im = coefficients[:, 0].astype(bf16), coefficients[:, 1].astype(bf16)
    packed_coeff = jnp.concatenate([c_re, -c_im, c_im, c_re], axis=1)
    rows_loc = coefficients.shape[0]
    u = basis_vectors.reshape(k_loc, side, side)
    d = strain.astype(bf16).reshape(cols * segs, side)
    vmem = pl.BlockSpec(memory_space=pltpu.VMEM)
    hbm = pl.BlockSpec(memory_space=pl.ANY)
    got, coeff_table = pl.pallas_call(
        functools.partial(exchange, n, group, segs),
        out_shape=[jax.ShapeDtypeStruct((n, 2, res, cols, wide), bf16),
                   jax.ShapeDtypeStruct((n, rows_loc, 4 * n_k), bf16)],
        in_specs=[vmem] * 6,
        out_specs=[hbm, hbm],
        scratch_shapes=[
            pltpu.VMEM((layers, layers, group, k_loc, cols, side), bf16),
            pltpu.VMEM((layers, cols * segs, side), bf16),
            pltpu.VMEM((n_k * cols, half), f32),
            pltpu.VMEM((n_k * cols, half), f32),
            pltpu.VMEM((2, group * res * cols, wide), f32),
            pltpu.VMEM((layers, 2, group * res, cols, wide), bf16),
            pltpu.VMEM((2 * group * res, side), bf16),
            pltpu.VMEM((2 * group * res, side), bf16),
        ] + [pltpu.SemaphoreType.DMA(dims) for dims in (
            (group, layers), (group, layers), (layers, layers, 2), (layers, layers), (layers, 2), (layers,),
            (n,), (n,), (group, layers), (group, layers), (3, layers))],
        compiler_params=pltpu.CompilerParams(collective_id=0, has_side_effects=True),
    )(u, d, packed_coeff, first_hi, first_lo, turn)
    tile = 8
    return pl.pallas_call(
        functools.partial(rebuild_kernel, segs),
        grid=(res // tile, segs),
        out_shape=jax.ShapeDtypeStruct((segs, templates, res, side), f32),
        in_specs=[vmem] * 5,
        out_specs=hbm,
        scratch_shapes=[
            pltpu.VMEM((segs, res, 2 * n_k, side), bf16),
            pltpu.VMEM((2 * templates, 2 * n_k), bf16),
            pltpu.VMEM((2, side // 128, templates * tile, 128), f32),
            pltpu.SemaphoreType.DMA((2, side // 128)),
        ],
    )(got, coeff_table.reshape(n * rows_loc, 4 * n_k), template_rows[None], second_hi, second_lo)


def solution(mesh):
    in_specs = (
        P("basis", None, None, None),
        P(("bank", "basis"), None, None, None),
        P(("bank", "basis"), None, None),
        P("bank"),
    )
    out_specs = P(None, "bank", "basis", None)
    return jax.shard_map(functools.partial(shards, mesh.shape["basis"]), mesh=mesh, in_specs=in_specs, out_specs=out_specs, check_vma=False)
```

```python
import functools
import math

import jax
import jax.numpy as jnp
import numpy as np
from jax import lax
from jax.experimental import pallas as pl
from jax.experimental.pallas import tpu as pltpu
from jax.sharding import PartitionSpec as P

highest = lax.Precision.HIGHEST


def rotation(left_index, right_index, period):
    turns = left_index * right_index % period
    angle = turns.astype(jnp.float32) * (2.0 * math.pi / period)
    return (jnp.cos(angle), jnp.sin(angle))


def complex_einsum(form, left_re, left_im, right_re, right_im):
    real_out = jnp.einsum(form, left_re, right_re, precision=highest) - jnp.einsum(
        form, left_im, right_im, precision=highest
    )
    imag_out = jnp.einsum(form, left_re, right_im, precision=highest) + jnp.einsum(
        form, left_im, right_re, precision=highest
    )
    return (real_out, imag_out)


def stack_rows(coeff_table, template_rows):
    chosen = coeff_table[template_rows].astype(jnp.bfloat16)
    return jnp.concatenate([chosen[:, 0], chosen[:, 1]], axis=0)


def rebuild(stacked, series_re, series_im):
    templates = stacked.shape[0] // 2
    left_sum = jnp.einsum("jk,sktu->sjtu", stacked, series_re, preferred_element_type=jnp.float32)
    right_sum = jnp.einsum("jk,sktu->sjtu", stacked, series_im, preferred_element_type=jnp.float32)
    rho_re = left_sum[:, :templates] - right_sum[:, templates:]
    rho_im = right_sum[:, :templates] + left_sum[:, templates:]
    return rho_re * rho_re + rho_im * rho_im


def shards_general(strain, basis_vectors, coefficients, template_rows):
    half_rows = strain.shape[3]
    side_len = 2 * half_rows
    samples = side_len * side_len
    freq_index = lax.broadcasted_iota(jnp.int32, (half_rows, side_len), 0)
    time_index = lax.broadcasted_iota(jnp.int32, (half_rows, side_len), 1)
    first_cos, first_sin = rotation(freq_index, time_index, side_len)
    column_index = lax.broadcasted_iota(jnp.int32, (side_len, side_len), 0)
    block_index = lax.broadcasted_iota(jnp.int32, (side_len, side_len), 1)
    second_cos, second_sin = rotation(column_index, block_index, side_len)
    coeff_table, whole_strain = (
        lax.all_gather(coefficients, "basis", axis=0, tiled=True),
        lax.all_gather(strain, "basis", axis=0, tiled=True),
    )
    stacked = stack_rows(coeff_table, template_rows)
    widened = basis_vectors.astype(jnp.float32)
    basis_re = widened[:, :, 0][None]
    basis_im = widened[:, :, 1][None]
    strain_re = jnp.transpose(whole_strain[:, :, 0], (1, 0, 2))[:, None]
    strain_im = jnp.transpose(whole_strain[:, :, 1], (1, 0, 2))[:, None]
    prod_re = basis_re * strain_re + basis_im * strain_im
    prod_im = basis_re * strain_im - basis_im * strain_re
    section_re, section_im = complex_einsum("skcr,rt->skct", prod_re, prod_im, first_cos, first_sin)
    twist_cos, twist_sin = rotation(column_index, block_index, samples)
    turned_re = section_re * twist_cos - section_im * twist_sin
    turned_im = section_re * twist_sin + section_im * twist_cos
    series_re, series_im = complex_einsum(
        "skct,cu->sktu", turned_re, turned_im, second_cos, second_sin
    )
    series_re = series_re.astype(jnp.bfloat16)
    series_im = series_im.astype(jnp.bfloat16)
    return rebuild(
        stacked,
        lax.all_to_all(series_re, "basis", split_axis=2, concat_axis=1, tiled=True),
        lax.all_to_all(series_im, "basis", split_axis=2, concat_axis=1, tiled=True),
    )


bf16 = jnp.bfloat16
f32 = jnp.float32
NT = (((1,), (1,)), ((), ()))
TN = (((0,), (0,)), ((), ()))


def split(values):
    high = values.astype(bf16)
    return high, (values - high.astype(f32)).astype(bf16)


def table(rows, columns, period):
    turns = np.outer(np.arange(rows), np.arange(columns)) % period
    angle = turns * (2.0 * math.pi / period)
    return np.cos(angle), np.sin(angle)


def halves(values):
    values = values.astype(np.float32)
    high = values.astype(bf16)
    return high, (values - high.astype(np.float32)).astype(bf16)


def exchange(n, group, segs, u_ref, strain_ref, coeff_ref, first_hi, first_lo, turn_ref, got_ref, table_ref,
             u_all, strain_all, wide_re, wide_im, sect, packed, left_hi, left_lo,
             send_u, recv_u, send_z, recv_z, send_d, recv_d, send_c, recv_c, send_s, recv_s, own_sem):
    me = lax.axis_index("basis")
    layers = n // group
    layer = me // group
    lane = lax.rem(me, group)
    k_loc, side = u_ref.shape[0], u_ref.shape[1]
    cols = side // n
    half = side // 2
    n_k = k_loc * n
    res = side // n
    near = group * res

    def remote(src, dst, send, recv, peer):
        return pltpu.make_async_remote_copy(src, dst, send, recv, device_id={"basis": peer},
                                            device_id_type=pl.DeviceIdType.MESH)

    def mate(off):
        return lax.rem(lane + off, group)

    def columns(q, owner):
        return pl.ds(pl.multiple_of((q * group + owner) * cols, cols), cols)

    def swap_u(off, q):
        to = mate(off)
        return remote(u_ref.at[:, columns(q, to)], u_all.at[q, layer, lane], send_u.at[off, q], recv_u.at[off, q],
                      layer * group + to)

    def swap_s(off, q):
        to = mate(off)
        rows = pl.ds(pl.multiple_of(to * res, res), res)
        return remote(packed.at[q, :, rows], got_ref.at[q * group + lane], send_s.at[off, q], recv_s.at[off, q],
                      layer * group + to)

    def keep_u(q):
        return pltpu.make_async_copy(u_ref.at[:, columns(q, lane)], u_all.at[q, layer, lane], own_sem.at[0, q])

    def keep_s(q):
        rows = pl.ds(pl.multiple_of(lane * res, res), res)
        return pltpu.make_async_copy(packed.at[q, :, rows], got_ref.at[q * group + lane], own_sem.at[1, q])

    def pass_u(q, origin, way):
        return remote(u_all.at[q, origin], u_all.at[q, origin], send_z.at[q, origin, way], recv_z.at[q, origin],
                      me + (2 * way - 1) * group)

    def pass_d(origin, way):
        return remote(strain_all.at[origin], strain_all.at[origin], send_d.at[origin, way], recv_d.at[origin],
                      me + (2 * way - 1) * group)

    def share_c(off):
        return remote(coeff_ref, table_ref.at[me], send_c.at[off], recv_c.at[off], lax.rem(me + off, n))

    def towards(way):
        return layer < layers - 1 if way else layer > 0

    def relay(q, dist):
        for way in range(2):
            origin = layer - dist if way else layer + dist

            @pl.when((origin >= 0) & (origin < layers))
            def _():
                @pl.when(origin == q)
                def _():
                    pass_d(origin, 0).wait_recv()

                    @pl.when(towards(way))
                    def _():
                        pass_d(origin, way).start()

                pass_u(q, origin, 0).wait_recv()

                @pl.when(towards(way))
                def _():
                    pass_u(q, origin, way).start()

    def drain(copy_of):
        for origin in range(layers):
            for way in range(2):
                sent = origin <= layer if way else origin >= layer

                @pl.when(towards(way) & sent)
                def _():
                    copy_of(origin, way).wait_send()

    def launch(q):
        keep_u(q).wait()
        for off in range(1, group):
            swap_u(off, q).wait_recv()
        for way in range(2):
            @pl.when(towards(way) & (layer == q))
            def _():
                pass_d(layer, way).start()

            @pl.when(towards(way))
            def _():
                pass_u(q, layer, way).start()

    barrier = pltpu.get_barrier_semaphore()
    for off in range(1, n):
        pl.semaphore_signal(barrier, inc=1, device_id={"basis": lax.rem(me + off, n)},
                            device_id_type=pl.DeviceIdType.MESH)
    own_d = pltpu.make_async_copy(strain_ref, strain_all.at[layer], own_sem.at[2, 0])
    own_d.start()
    own_c = pltpu.make_async_copy(coeff_ref, table_ref.at[me], own_sem.at[2, 1])
    own_c.start()
    for q in range(layers):
        keep_u(q).start()
    own_d.wait()
    pl.semaphore_wait(barrier, n - 1)
    for q in range(layers):
        for off in range(1, group):
            swap_u(off, q).start()
    for part in range(2):
        rows = pl.ds(pl.multiple_of(part * side + layer * near, near), near)
        left_hi[part * near:(part + 1) * near, :] = first_hi[rows, :]
        left_lo[part * near:(part + 1) * near, :] = first_lo[rows, :]
    launch(0)
    launch(1)
    for stage in range(1, layers - 1):
        for dist in range(1, stage + 1):
            relay(stage - dist, dist)
        launch(stage + 1)
    for off in range(1, n):
        share_c(off).start()

    @pl.loop(0, layers)
    def _(q):
        for dist in range(1, layers):
            chunk = q + layers - 1 - dist

            @pl.when(chunk < layers)
            def _():
                relay(chunk, dist)

        wide = u_all[q].astype(f32).reshape(n_k * cols, side)
        wide_re[...] = wide[:, :half]
        wide_im[...] = wide[:, half:]
        turn = turn_ref[q]
        strain_q = strain_all[q].astype(f32)
        for c in range(cols):
            u_re = wide_re[pl.ds(c, n_k, stride=cols), :]
            u_im = wide_im[pl.ds(c, n_k, stride=cols), :]
            parts = []
            for s in range(segs):
                row = c * segs + s
                d_re, d_im = strain_q[row:row + 1, :half], strain_q[row:row + 1, half:]
                parts.append(jnp.concatenate([u_re * d_re + u_im * d_im, u_re * d_im - u_im * d_re], axis=1))
            high, low = split(jnp.concatenate(parts, axis=0))
            out = lax.dot_general(left_hi[...], high, NT, preferred_element_type=f32)
            out += lax.dot_general(left_lo[...], high, NT, preferred_element_type=f32)
            out += lax.dot_general(left_hi[...], low, NT, preferred_element_type=f32)
            t_cos = turn[:, c:c + 1]
            t_sin = turn[:, cols + c:cols + c + 1]
            o_re, o_im = out[:near], out[near:]
            sect[0, pl.ds(c, near, stride=cols), :] = o_re * t_cos - o_im * t_sin
            sect[1, pl.ds(c, near, stride=cols), :] = o_re * t_sin + o_im * t_cos
        packed[q] = sect[...].astype(bf16).reshape(packed.shape[1:])
        for off in range(1, group):
            swap_s(off, q).start()
        keep_s(q).start()

    own_c.wait()
    for off in range(1, n):
        share_c(off).wait()
    drain(pass_d)

    @pl.loop(0, layers)
    def _(q):
        drain(functools.partial(pass_u, q))
        keep_s(q).wait()
        for off in range(1, group):
            swap_u(off, q).wait_send()
            swap_s(off, q).wait()


def rebuild_kernel(segs, got_ref, table_ref, rows_ref, second_hi, second_lo, out_ref, series, left, stage, out_sem):
    n, _, res, cols, wide = got_ref.shape
    side = n * cols
    n_k = wide // segs
    templates = rows_ref.shape[1]
    tile = stage.shape[2] // templates
    batch = tile // 2
    step_a, step_s = pl.program_id(0), pl.program_id(1)
    step = step_a * segs + step_s
    slot = lax.rem(step, 2)

    def writes(at_slot, at_a, at_s):
        span = pl.ds(pl.multiple_of(at_a * tile, tile), tile)
        return [pltpu.make_async_copy(stage.at[at_slot, h].reshape(templates, tile, 128),
                                      out_ref.at[at_s, :, span, pl.ds(h * 128, 128)],
                                      out_sem.at[at_slot, h]) for h in range(side // 128)]

    def second(first):
        both = []
        for part in range(2):
            block = jnp.concatenate([got_ref[:, part, first + i].reshape(side, wide) for i in range(batch)], axis=1)
            both.append(lax.dot_general(block, second_hi[...], TN, preferred_element_type=f32)
                        + lax.dot_general(block, second_lo[...], TN, preferred_element_type=f32))
        z_re = (both[0][:, :side] - both[1][:, side:]).astype(bf16)
        z_im = (both[0][:, side:] + both[1][:, :side]).astype(bf16)
        for i in range(batch):
            for s in range(segs):
                rows = slice(i * wide + s * n_k, i * wide + (s + 1) * n_k)
                series[s, first + i, :n_k] = z_re[rows]
                series[s, first + i, n_k:] = z_im[rows]

    @pl.when(step == 0)
    def _():
        index = lax.broadcasted_iota(jnp.int32, (table_ref.shape[0], templates), 0)
        hot = jnp.where(index == rows_ref[...], 1.0, 0.0).astype(bf16)
        picked = lax.dot_general(hot, table_ref[...], TN, preferred_element_type=f32).astype(bf16)
        left[:templates] = picked[:, :2 * n_k]
        left[templates:] = picked[:, 2 * n_k:]

        @pl.loop(0, 2)
        def _(i):
            second(i * batch)

    @pl.when((step_s < 2) & (step_a < pl.num_programs(0) - 1))
    def _():
        second((step_a + 1) * tile + step_s * batch)

    @pl.when(step >= 2)
    def _():
        for copy in writes(slot, 0, 0):
            copy.wait()

    for a in range(tile):
        rho = jnp.dot(left[...], series[step_s, step_a * tile + a], preferred_element_type=f32)
        p_re, p_im = rho[:templates], rho[templates:]
        power = p_re * p_re + p_im * p_im
        for h in range(side // 128):
            stage[slot, h, pl.ds(a, templates, stride=tile), :] = power[:, h * 128:(h + 1) * 128]
    for copy in writes(slot, step_a, step_s):
        copy.start()

    @pl.when(step == pl.num_programs(0) * segs - 1)
    def _():
        for at_slot in range(2):
            for copy in writes(at_slot, 0, 0):
                copy.wait()


def shards(n, strain, basis_vectors, coefficients, template_rows):
    cols, segs, _, half = strain.shape
    side = 2 * half
    k_loc = basis_vectors.shape[0]
    n_k = k_loc * n
    res = side // n
    templates = template_rows.shape[0]
    wide = segs * n_k
    if cols % 16 or segs < 2 or wide != 128 or n_k % 16 or coefficients.shape[0] % 16 or math.isqrt(n) ** 2 != n:
        return shards_general(strain, basis_vectors, coefficients, template_rows)
    samples = side * side
    cos1, sin1 = table(side, half, side)
    first_hi, first_lo = halves(np.block([[cos1, -sin1], [sin1, cos1]]))
    cos2, sin2 = table(side, side, side)
    second_hi, second_lo = halves(np.concatenate([cos2, sin2], axis=1))
    me = lax.axis_index("basis")
    group = math.isqrt(n)
    layers = n // group
    grid = (layers, group * res, cols)
    lane = me % group
    column = (lax.broadcasted_iota(jnp.int32, grid, 0) * group + lane) * cols + lax.broadcasted_iota(jnp.int32, grid, 2)
    residue = me // group * group * res + lax.broadcasted_iota(jnp.int32, grid, 1)
    angle = (column * residue % samples).astype(f32) * (2.0 * math.pi / samples)
    turn = jnp.concatenate([jnp.cos(angle), jnp.sin(angle)], axis=2)
    c_re, c_im = coefficients[:, 0].astype(bf16), coefficients[:, 1].astype(bf16)
    packed_coeff = jnp.concatenate([c_re, -c_im, c_im, c_re], axis=1)
    rows_loc = coefficients.shape[0]
    u = basis_vectors.reshape(k_loc, side, side)
    d = strain.astype(bf16).reshape(cols * segs, side)
    vmem = pl.BlockSpec(memory_space=pltpu.VMEM)
    hbm = pl.BlockSpec(memory_space=pl.ANY)
    got, coeff_table = pl.pallas_call(
        functools.partial(exchange, n, group, segs),
        out_shape=[jax.ShapeDtypeStruct((n, 2, res, cols, wide), bf16),
                   jax.ShapeDtypeStruct((n, rows_loc, 4 * n_k), bf16)],
        in_specs=[vmem] * 6,
        out_specs=[hbm, hbm],
        scratch_shapes=[
            pltpu.VMEM((layers, layers, group, k_loc, cols, side), bf16),
            pltpu.VMEM((layers, cols * segs, side), bf16),
            pltpu.VMEM((n_k * cols, half), f32),
            pltpu.VMEM((n_k * cols, half), f32),
            pltpu.VMEM((2, group * res * cols, wide), f32),
            pltpu.VMEM((layers, 2, group * res, cols, wide), bf16),
            pltpu.VMEM((2 * group * res, side), bf16),
            pltpu.VMEM((2 * group * res, side), bf16),
        ] + [pltpu.SemaphoreType.DMA(dims) for dims in (
            (group, layers), (group, layers), (layers, layers, 2), (layers, layers), (layers, 2), (layers,),
            (n,), (n,), (group, layers), (group, layers), (3, layers))],
        compiler_params=pltpu.CompilerParams(collective_id=0, has_side_effects=True),
    )(u, d, packed_coeff, first_hi, first_lo, turn)
    tile = 8
    return pl.pallas_call(
        functools.partial(rebuild_kernel, segs),
        grid=(res // tile, segs),
        out_shape=jax.ShapeDtypeStruct((segs, templates, res, side), f32),
        in_specs=[vmem] * 5,
        out_specs=hbm,
        scratch_shapes=[
            pltpu.VMEM((segs, res, 2 * n_k, side), bf16),
            pltpu.VMEM((2 * templates, 2 * n_k), bf16),
            pltpu.VMEM((2, side // 128, templates * tile, 128), f32),
            pltpu.SemaphoreType.DMA((2, side // 128)),
        ],
    )(got, coeff_table.reshape(n * rows_loc, 4 * n_k), template_rows[None], second_hi, second_lo)


def solution(mesh):
    in_specs = (
        P("basis", None, None, None),
        P(("bank", "basis"), None, None, None),
        P(("bank", "basis"), None, None),
        P("bank"),
    )
    out_specs = P(None, "bank", "basis", None)
    return jax.shard_map(functools.partial(shards, mesh.shape["basis"]), mesh=mesh, in_specs=in_specs, out_specs=out_specs, check_vma=False)
```

```python
import functools
import math

import jax
import jax.numpy as jnp
import numpy as np
from jax import lax
from jax.experimental import pallas as pl
from jax.experimental.pallas import tpu as pltpu
from jax.sharding import PartitionSpec as P

highest = lax.Precision.HIGHEST


def rotation(left_index, right_index, period):
    turns = left_index * right_index % period
    angle = turns.astype(jnp.float32) * (2.0 * math.pi / period)
    return (jnp.cos(angle), jnp.sin(angle))


def complex_einsum(form, left_re, left_im, right_re, right_im):
    real_out = jnp.einsum(form, left_re, right_re, precision=highest) - jnp.einsum(
        form, left_im, right_im, precision=highest
    )
    imag_out = jnp.einsum(form, left_re, right_im, precision=highest) + jnp.einsum(
        form, left_im, right_re, precision=highest
    )
    return (real_out, imag_out)


def stack_rows(coeff_table, template_rows):
    chosen = coeff_table[template_rows].astype(jnp.bfloat16)
    return jnp.concatenate([chosen[:, 0], chosen[:, 1]], axis=0)


def rebuild(stacked, series_re, series_im):
    templates = stacked.shape[0] // 2
    left_sum = jnp.einsum("jk,sktu->sjtu", stacked, series_re, preferred_element_type=jnp.float32)
    right_sum = jnp.einsum("jk,sktu->sjtu", stacked, series_im, preferred_element_type=jnp.float32)
    rho_re = left_sum[:, :templates] - right_sum[:, templates:]
    rho_im = right_sum[:, :templates] + left_sum[:, templates:]
    return rho_re * rho_re + rho_im * rho_im


def shards_general(strain, basis_vectors, coefficients, template_rows):
    half_rows = strain.shape[3]
    side_len = 2 * half_rows
    samples = side_len * side_len
    freq_index = lax.broadcasted_iota(jnp.int32, (half_rows, side_len), 0)
    time_index = lax.broadcasted_iota(jnp.int32, (half_rows, side_len), 1)
    first_cos, first_sin = rotation(freq_index, time_index, side_len)
    column_index = lax.broadcasted_iota(jnp.int32, (side_len, side_len), 0)
    block_index = lax.broadcasted_iota(jnp.int32, (side_len, side_len), 1)
    second_cos, second_sin = rotation(column_index, block_index, side_len)
    coeff_table, whole_strain = (
        lax.all_gather(coefficients, "basis", axis=0, tiled=True),
        lax.all_gather(strain, "basis", axis=0, tiled=True),
    )
    stacked = stack_rows(coeff_table, template_rows)
    widened = basis_vectors.astype(jnp.float32)
    basis_re = widened[:, :, 0][None]
    basis_im = widened[:, :, 1][None]
    strain_re = jnp.transpose(whole_strain[:, :, 0], (1, 0, 2))[:, None]
    strain_im = jnp.transpose(whole_strain[:, :, 1], (1, 0, 2))[:, None]
    prod_re = basis_re * strain_re + basis_im * strain_im
    prod_im = basis_re * strain_im - basis_im * strain_re
    section_re, section_im = complex_einsum("skcr,rt->skct", prod_re, prod_im, first_cos, first_sin)
    twist_cos, twist_sin = rotation(column_index, block_index, samples)
    turned_re = section_re * twist_cos - section_im * twist_sin
    turned_im = section_re * twist_sin + section_im * twist_cos
    series_re, series_im = complex_einsum(
        "skct,cu->sktu", turned_re, turned_im, second_cos, second_sin
    )
    series_re = series_re.astype(jnp.bfloat16)
    series_im = series_im.astype(jnp.bfloat16)
    return rebuild(
        stacked,
        lax.all_to_all(series_re, "basis", split_axis=2, concat_axis=1, tiled=True),
        lax.all_to_all(series_im, "basis", split_axis=2, concat_axis=1, tiled=True),
    )


bf16 = jnp.bfloat16
f32 = jnp.float32
NT = (((1,), (1,)), ((), ()))
TN = (((0,), (0,)), ((), ()))


def split(values):
    high = values.astype(bf16)
    return high, (values - high.astype(f32)).astype(bf16)


def table(rows, columns, period):
    turns = np.outer(np.arange(rows), np.arange(columns)) % period
    angle = turns * (2.0 * math.pi / period)
    return np.cos(angle), np.sin(angle)


def halves(values):
    values = values.astype(np.float32)
    high = values.astype(bf16)
    return high, (values - high.astype(np.float32)).astype(bf16)


def exchange(n, group, segs, u_ref, strain_ref, coeff_ref, first_hi, first_lo, got_ref, table_ref,
             u_all, strain_all, wide, sect, packed, left_hi, left_lo,
             send_u, recv_u, send_z, recv_z, send_d, recv_d, send_c, recv_c, send_s, recv_s, own_sem):
    me = lax.axis_index("basis")
    layers = n // group
    layer = me // group
    lane = lax.rem(me, group)
    k_loc, side = u_ref.shape[0], u_ref.shape[1] // 2
    cols = side // n
    half = side // 2
    n_k = k_loc * n
    res = side // n
    near = group * res

    def remote(src, dst, send, recv, peer):
        return pltpu.make_async_remote_copy(src, dst, send, recv, device_id={"basis": peer},
                                            device_id_type=pl.DeviceIdType.MESH)

    def mate(off):
        return lax.rem(lane + off, group)

    def columns(q, owner):
        return pl.ds(pl.multiple_of((q * group + owner) * 2 * cols, 2 * cols), 2 * cols)

    def swap_u(off, q):
        to = mate(off)
        return remote(u_ref.at[:, columns(q, to)], u_all.at[q, layer, lane], send_u.at[off, q], recv_u.at[off, q],
                      layer * group + to)

    def swap_s(off, q):
        to = mate(off)
        rows = pl.ds(pl.multiple_of(to * res, res), res)
        return remote(packed.at[q, :, rows], got_ref.at[q * group + lane], send_s.at[off, q], recv_s.at[off, q],
                      layer * group + to)

    def keep_u(q):
        return pltpu.make_async_copy(u_ref.at[:, columns(q, lane)], u_all.at[q, layer, lane], own_sem.at[0, q])

    def keep_s(q):
        rows = pl.ds(pl.multiple_of(lane * res, res), res)
        return pltpu.make_async_copy(packed.at[q, :, rows], got_ref.at[q * group + lane], own_sem.at[1, q])

    def pass_u(q, origin, way):
        return remote(u_all.at[q, origin], u_all.at[q, origin], send_z.at[q, origin, way], recv_z.at[q, origin],
                      me + (2 * way - 1) * group)

    def pass_d(origin, way):
        return remote(strain_all.at[origin], strain_all.at[origin], send_d.at[origin, way], recv_d.at[origin],
                      me + (2 * way - 1) * group)

    def share_c(off):
        return remote(coeff_ref, table_ref.at[me], send_c.at[off], recv_c.at[off], lax.rem(me + off, n))

    def towards(way):
        return layer < layers - 1 if way else layer > 0

    def relay(q, dist):
        for way in range(2):
            origin = layer - dist if way else layer + dist

            @pl.when((origin >= 0) & (origin < layers))
            def _():
                @pl.when(origin == q)
                def _():
                    pass_d(origin, 0).wait_recv()

                    @pl.when(towards(way))
                    def _():
                        pass_d(origin, way).start()

                pass_u(q, origin, 0).wait_recv()

                @pl.when(towards(way))
                def _():
                    pass_u(q, origin, way).start()

    def drain(copy_of):
        for origin in range(layers):
            for way in range(2):
                sent = origin <= layer if way else origin >= layer

                @pl.when(towards(way) & sent)
                def _():
                    copy_of(origin, way).wait_send()

    def launch(q):
        keep_u(q).wait()
        for off in range(1, group):
            swap_u(off, q).wait_recv()
        for way in range(2):
            @pl.when(towards(way) & (layer == q))
            def _():
                pass_d(layer, way).start()

            @pl.when(towards(way))
            def _():
                pass_u(q, layer, way).start()

    barrier = pltpu.get_barrier_semaphore()
    for off in range(1, n):
        pl.semaphore_signal(barrier, inc=1, device_id={"basis": lax.rem(me + off, n)},
                            device_id_type=pl.DeviceIdType.MESH)
    strain_all[layer] = strain_ref[...].astype(bf16)
    own_c = pltpu.make_async_copy(coeff_ref, table_ref.at[me], own_sem.at[2, 0])
    own_c.start()
    for q in range(layers):
        keep_u(q).start()
    pl.semaphore_wait(barrier, n - 1)
    for q in range(layers):
        for off in range(1, group):
            swap_u(off, q).start()
    for part in range(2):
        rows = pl.ds(pl.multiple_of(part * side + layer * near, near), near)
        left_hi[part * near:(part + 1) * near, :] = first_hi[rows, :]
        left_lo[part * near:(part + 1) * near, :] = first_lo[rows, :]
    launch(0)
    launch(1)
    for stage in range(1, layers - 1):
        for dist in range(1, stage + 1):
            relay(stage - dist, dist)
        launch(stage + 1)
    for off in range(1, n):
        share_c(off).start()

    @pl.loop(0, layers)
    def _(q):
        for dist in range(1, layers):
            chunk = q + layers - 1 - dist

            @pl.when(chunk < layers)
            def _():
                relay(chunk, dist)

        wide[...] = u_all[q].astype(f32).reshape(wide.shape)
        column = (q * group + lane) * cols + lax.broadcasted_iota(jnp.int32, (near, cols), 1)
        residue = layer * near + lax.broadcasted_iota(jnp.int32, (near, cols), 0)
        angle = lax.rem(column * residue, side * side).astype(f32) * (2.0 * math.pi / (side * side))
        turn_cos, turn_sin = jnp.cos(angle), jnp.sin(angle)
        strain_q = strain_all[q].astype(f32)
        for c in range(cols):
            u_re = wide[pl.ds(2 * c, n_k, stride=2 * cols), :]
            u_im = wide[pl.ds(2 * c + 1, n_k, stride=2 * cols), :]
            parts = []
            for s in range(segs):
                row = 2 * (c * segs + s)
                d_re, d_im = strain_q[row:row + 1], strain_q[row + 1:row + 2]
                parts.append(jnp.concatenate([u_re * d_re + u_im * d_im, u_re * d_im - u_im * d_re], axis=1))
            high, low = split(jnp.concatenate(parts, axis=0))
            out = lax.dot_general(left_hi[...], high, NT, preferred_element_type=f32)
            out += lax.dot_general(left_lo[...], high, NT, preferred_element_type=f32)
            out += lax.dot_general(left_hi[...], low, NT, preferred_element_type=f32)
            t_cos = turn_cos[:, c:c + 1]
            t_sin = turn_sin[:, c:c + 1]
            o_re, o_im = out[:near], out[near:]
            sect[0, pl.ds(c, near, stride=cols), :] = o_re * t_cos - o_im * t_sin
            sect[1, pl.ds(c, near, stride=cols), :] = o_re * t_sin + o_im * t_cos
        packed[q] = sect[...].astype(bf16).reshape(packed.shape[1:])
        for off in range(1, group):
            swap_s(off, q).start()
        keep_s(q).start()

    own_c.wait()
    for off in range(1, n):
        share_c(off).wait()
    drain(pass_d)

    @pl.loop(0, layers)
    def _(q):
        drain(functools.partial(pass_u, q))
        keep_s(q).wait()
        for off in range(1, group):
            swap_u(off, q).wait_send()
            swap_s(off, q).wait()


def rebuild_kernel(segs, got_ref, table_ref, rows_ref, second_hi, second_lo, out_ref, series, left, stage, out_sem):
    n, _, res, cols, wide = got_ref.shape
    side = n * cols
    n_k = wide // segs
    templates = rows_ref.shape[1]
    tile = stage.shape[2] // templates
    batch = tile // 2
    step_a, step_s = pl.program_id(0), pl.program_id(1)
    step = step_a * segs + step_s
    slot = lax.rem(step, 2)

    def writes(at_slot, at_a, at_s):
        span = pl.ds(pl.multiple_of(at_a * tile, tile), tile)
        return [pltpu.make_async_copy(stage.at[at_slot, h].reshape(templates, tile, 128),
                                      out_ref.at[at_s, :, span, pl.ds(h * 128, 128)],
                                      out_sem.at[at_slot, h]) for h in range(side // 128)]

    def second(first):
        both = []
        for part in range(2):
            block = jnp.concatenate([got_ref[:, part, first + i].reshape(side, wide) for i in range(batch)], axis=1)
            both.append(lax.dot_general(block, second_hi[...], TN, preferred_element_type=f32)
                        + lax.dot_general(block, second_lo[...], TN, preferred_element_type=f32))
        z_re = (both[0][:, :side] - both[1][:, side:]).astype(bf16)
        z_im = (both[0][:, side:] + both[1][:, :side]).astype(bf16)
        for i in range(batch):
            for s in range(segs):
                rows = slice(i * wide + s * n_k, i * wide + (s + 1) * n_k)
                series[s, first + i, :n_k] = z_re[rows]
                series[s, first + i, n_k:] = z_im[rows]

    @pl.when(step == 0)
    def _():
        index = lax.broadcasted_iota(jnp.int32, (table_ref.shape[0], templates), 0)
        hot = jnp.where(index == rows_ref[...], 1.0, 0.0).astype(bf16)
        picked = lax.dot_general(hot, table_ref[...], TN, preferred_element_type=f32).astype(bf16)
        left[:templates] = picked[:, :2 * n_k]
        left[templates:] = picked[:, 2 * n_k:]

        @pl.loop(0, 2)
        def _(i):
            second(i * batch)

    @pl.when((step_s < 2) & (step_a < pl.num_programs(0) - 1))
    def _():
        second((step_a + 1) * tile + step_s * batch)

    @pl.when(step >= 2)
    def _():
        for copy in writes(slot, 0, 0):
            copy.wait()

    for a in range(tile):
        rho = jnp.dot(left[...], series[step_s, step_a * tile + a], preferred_element_type=f32)
        p_re, p_im = rho[:templates], rho[templates:]
        power = p_re * p_re + p_im * p_im
        for h in range(side // 128):
            stage[slot, h, pl.ds(a, templates, stride=tile), :] = power[:, h * 128:(h + 1) * 128]
    for copy in writes(slot, step_a, step_s):
        copy.start()

    @pl.when(step == pl.num_programs(0) * segs - 1)
    def _():
        for at_slot in range(2):
            for copy in writes(at_slot, 0, 0):
                copy.wait()


def shards(n, strain, basis_vectors, coefficients, template_rows):
    cols, segs, _, half = strain.shape
    side = 2 * half
    k_loc = basis_vectors.shape[0]
    n_k = k_loc * n
    res = side // n
    templates = template_rows.shape[0]
    wide = segs * n_k
    if cols % 16 or segs < 2 or wide != 128 or n_k % 16 or coefficients.shape[0] % 16 or math.isqrt(n) ** 2 != n:
        return shards_general(strain, basis_vectors, coefficients, template_rows)
    cos1, sin1 = table(side, half, side)
    first_hi, first_lo = halves(np.block([[cos1, -sin1], [sin1, cos1]]))
    cos2, sin2 = table(side, side, side)
    second_hi, second_lo = halves(np.concatenate([cos2, sin2], axis=1))
    me = lax.axis_index("basis")
    group = math.isqrt(n)
    layers = n // group
    c_re, c_im = coefficients[:, 0].astype(bf16), coefficients[:, 1].astype(bf16)
    packed_coeff = jnp.concatenate([c_re, -c_im, c_im, c_re], axis=1)
    rows_loc = coefficients.shape[0]
    u = basis_vectors.reshape(k_loc, 2 * side, half)
    d = strain.reshape(2 * cols * segs, half)
    vmem = pl.BlockSpec(memory_space=pltpu.VMEM)
    hbm = pl.BlockSpec(memory_space=pl.ANY)
    got, coeff_table = pl.pallas_call(
        functools.partial(exchange, n, group, segs),
        out_shape=[jax.ShapeDtypeStruct((n, 2, res, cols, wide), bf16),
                   jax.ShapeDtypeStruct((n, rows_loc, 4 * n_k), bf16)],
        in_specs=[vmem] * 5,
        out_specs=[hbm, hbm],
        scratch_shapes=[
            pltpu.VMEM((layers, layers, group, k_loc, 2 * cols, half), bf16),
            pltpu.VMEM((layers, 2 * cols * segs, half), bf16),
            pltpu.VMEM((2 * n_k * cols, half), f32),
            pltpu.VMEM((2, group * res * cols, wide), f32),
            pltpu.VMEM((layers, 2, group * res, cols, wide), bf16),
            pltpu.VMEM((2 * group * res, side), bf16),
            pltpu.VMEM((2 * group * res, side), bf16),
        ] + [pltpu.SemaphoreType.DMA(dims) for dims in (
            (group, layers), (group, layers), (layers, layers, 2), (layers, layers), (layers, 2), (layers,),
            (n,), (n,), (group, layers), (group, layers), (3, layers))],
        compiler_params=pltpu.CompilerParams(collective_id=0, has_side_effects=True),
    )(u, d, packed_coeff, first_hi, first_lo)
    tile = 8
    return pl.pallas_call(
        functools.partial(rebuild_kernel, segs),
        grid=(res // tile, segs),
        out_shape=jax.ShapeDtypeStruct((segs, templates, res, side), f32),
        in_specs=[vmem] * 5,
        out_specs=hbm,
        scratch_shapes=[
            pltpu.VMEM((segs, res, 2 * n_k, side), bf16),
            pltpu.VMEM((2 * templates, 2 * n_k), bf16),
            pltpu.VMEM((2, side // 128, templates * tile, 128), f32),
            pltpu.SemaphoreType.DMA((2, side // 128)),
        ],
    )(got, coeff_table.reshape(n * rows_loc, 4 * n_k), template_rows[None], second_hi, second_lo)


def solution(mesh):
    in_specs = (
        P("basis", None, None, None),
        P(("bank", "basis"), None, None, None),
        P(("bank", "basis"), None, None),
        P("bank"),
    )
    out_specs = P(None, "bank", "basis", None)
    return jax.shard_map(functools.partial(shards, mesh.shape["basis"]), mesh=mesh, in_specs=in_specs, out_specs=out_specs, check_vma=False)
```
